32 devices in a mesh: mem: 4 (over z), tile: 8 (over y, x, core).
Axes of the slice: x: 2, y: 2, z: 4, core: 2. Of those that a mesh axis runs over, the one named last changes fastest.
Arguments:
- alpha: float32 [32, 8, 192, 384], P('mem', None, 'tile'), may hold values from -6 to 6
- ensemble: bfloat16 [2, 32, 8, 192, 384], P(None, 'mem', None, 'tile'), may hold values from -1 to 1
- innovation: float32 [2, 8, 192, 384], P(None, None, 'tile'), may hold values from -6 to 6
- precision: float32 [2, 8, 192, 384], P(None, None, 'tile'), may hold values from 0.5 to 8
- diffusivity: float32 [2, 8, 192, 384], P(None, None, 'tile'), may hold values from 0.01 to 0.48, as said below
Outputs:
- gradient: float32 [32, 8, 192, 384], P('mem', None, 'tile')
- increment: float32 [2, 8, 192, 384], P(None, None, 'tile')
The draws below stay inside these ranges and needn't reach their ends.
Inputs may be any that keep to these rules, and one draw needn't show every extreme that they name: diffusivity[0] lies between 0.40 and 0.48 and diffusivity[1] between 0.01 and 0.02, so the four faces of a cell sum to at most 1.
All inputs are finite; a program needn't handle non-finite values.
Results may differ from the reference program's by a relative error of at most 0.0003.
Values sent between devices are 32-bit elements; how exact they have to be, the bound alone decides.
A program may use at most 64 MiB of HBM per device.

```python
import math
import jax
import jax.numpy as jnp
from jax import lax

NROW = 384
LEVELS = 8
SLOTS = 2
STEPS = 4
MEMBERS = 32
NCOL = 192


def draw_diffusivity(key, part):
    zonal_key = jax.random.fold_in(key, 101)
    merid_key = jax.random.fold_in(key, 202)
    zonal_low = 0.4
    zonal = jax.random.uniform(zonal_key, (1, LEVELS, NCOL, NROW), jnp.float32, zonal_low, 0.48)
    merid = jax.random.uniform(merid_key, (1, LEVELS, NCOL, NROW), jnp.float32, 0.01, 0.02)
    return jnp.concatenate([zonal, merid], axis=0)


def block_levels(own_key, dims, pieces, smallest, high):
    def one(position, parts):
        heights = jax.random.uniform(jax.random.fold_in(jax.random.fold_in(own_key, 6), position), (parts,), jnp.float32, smallest / len(pieces), high / len(pieces))
        return jnp.repeat(jnp.exp(heights), dims[position] // parts).reshape((-1,) + (1,) * (len(dims) - position - 1))

    level = one(*pieces[0])
    for cut in pieces[1:]:
        level = level * one(*cut)
    return level


def scatter_about(own_key, shape, scale, reach, cuts=(), kind=jnp.bfloat16):
    loudness = block_levels(own_key, shape, cuts, -0.22, 0.18) if cuts else 1.0
    entries = jax.random.normal(own_key, shape, jnp.float32) * scale * loudness
    return jnp.minimum(jnp.maximum(entries, -reach), reach).astype(kind)


def setup_inputs(seed: int = 0) -> dict:
    keys = jax.random.split(jax.random.key(seed), 6)
    return {
        "alpha": scatter_about(keys[0], (MEMBERS, LEVELS, NCOL, NROW), 1.0, 6.0, ((0, 4), (2, 8)), jnp.float32),
        "ensemble": scatter_about(keys[1], (SLOTS, MEMBERS, LEVELS, NCOL, NROW), MEMBERS ** -0.5, 1.0, ((1, 4), (3, 8))),
        "innovation": scatter_about(keys[2], (SLOTS, LEVELS, NCOL, NROW), 1.0, 6.0, ((2, 8),), jnp.float32),
        "precision": jnp.clip(jnp.exp(math.log(8.0) - 2.7725887 * jax.random.uniform(keys[3], (SLOTS, LEVELS, NCOL, NROW), jnp.float32) ** block_levels(keys[3], (SLOTS, LEVELS, NCOL, NROW), ((2, 8),), -0.2, 0.2)), 0.5, 8.0),
        "diffusivity": draw_diffusivity(jax.random.fold_in(keys[5], 71), 0),
    }


def diffuse_step(field, diffusivity):
    east = jnp.roll(field, -1, axis=1)
    zonal_flux = diffusivity[0] * (east - field)
    merid_flux = diffusivity[1][:, :, :-1] * (field[:, :, 1:] - field[:, :, :-1])
    padding = jnp.zeros_like(field[:, :, :1])
    north_flux = jnp.concatenate([merid_flux, padding], axis=2)
    south_flux = jnp.concatenate([padding, merid_flux], axis=2)
    return field + zonal_flux - jnp.roll(zonal_flux, 1, axis=1) + north_flux - south_flux

def localize(field, diffusivity):
    for sweep in range(STEPS):
        field = diffuse_step(field, diffusivity)
    return field

def reference(alpha, ensemble, innovation, precision, diffusivity):
    members_first = jnp.swapaxes(ensemble, 0, 1)

    def accumulate(total, items):
        control, perturb = items
        localized = localize(control, diffusivity)
        return (total + perturb.astype(jnp.float32) * localized[None], None)
    start = jnp.zeros(innovation.shape, jnp.float32)
    increment, unused = lax.scan(accumulate, start, (alpha, members_first))
    weighted = precision * (increment - innovation)

    def member_grad(items):
        control, perturb = items
        projected = lax.optimization_barrier(jnp.sum(perturb.astype(jnp.float32) * weighted, axis=0))
        return control + localize(projected, diffusivity)
    gradient = lax.map(member_grad, (alpha, members_first))
    return (gradient, increment)
```

```python
import functools

import jax
import jax.numpy as jnp
from jax import lax
from jax.experimental import pallas as pl
from jax.experimental.pallas import tpu as pltpu
from jax.sharding import PartitionSpec as P

STEPS = 4
LAG_PAIR, LAG_TOTAL, LAG_PROJECT, LAG_ADJOINT = 1, 2, 4, 6
MESH = pl.DeviceIdType.MESH


def diffuse(field, zonal, merid):
    columns, rows = field.shape
    for _ in range(STEPS):
        zonal_flux = zonal * (pltpu.roll(field, columns - 1, 0) - field)
        merid_flux = merid * (pltpu.roll(field, rows - 1, 1) - field)
        field = (
            (field + zonal_flux)
            - pltpu.roll(zonal_flux, 1, 0)
            + (merid_flux - pltpu.roll(merid_flux, 1, 1))
        )
    return field


def kernel(
    tiles, alpha, ens, innov, prec, diff, grad, inc,
    av, ev, iv, pv, dv, pj, part, r1, r2, tot,
    a_send, a_recv, d_send, d_recv, p_send, p_recv,
    r1_send, r1_recv, r2_send, r2_recv, t_send, t_recv,
    a_sem, e_sem, d_sem, i_sem, w_sem, g_sem, n_sem,
):
    members, levels, cols, rows = alpha.shape
    z = lax.axis_index("mem")
    t = lax.axis_index("tile")
    right, left = lax.rem(t + 1, tiles), lax.rem(t + tiles - 1, tiles)
    inner = (z == 1) | (z == 2)
    outer = (z == 0) | (z == 3)
    partner = z + 1 - 2 * lax.rem(z, 2)
    across = 3 - z

    def remote(src, dst, send, recv, where):
        return pltpu.make_async_remote_copy(
            src_ref=src, dst_ref=dst, send_sem=send, recv_sem=recv,
            device_id=where, device_id_type=MESH,
        )

    def halo(src, dst, send, recv, l):
        return (
            remote(src.at[:, l, 0:STEPS], dst.at[:, l, cols:cols + STEPS],
                   send.at[0, l], recv.at[0, l], {"tile": left}),
            remote(src.at[:, l, cols - STEPS:cols], dst.at[:, l, cols + STEPS:cols + 2 * STEPS],
                   send.at[1, l], recv.at[1, l], {"tile": right}),
        )

    def alpha_halo(l):
        return halo(alpha, av, a_send, a_recv, l)

    def diff_halo(l):
        return halo(diff, dv, d_send, d_recv, l)

    def proj_halo(l):
        return halo(pj, pj, p_send, p_recv, l)

    def local(l):
        return (
            pltpu.make_async_copy(diff.at[:, l], dv.at[:, l, 0:cols], d_sem.at[l]),
            pltpu.make_async_copy(alpha.at[:, l], av.at[:, l, 0:cols], a_sem.at[l]),
            pltpu.make_async_copy(ens.at[:, :, l], ev.at[:, :, l], e_sem.at[l]),
        )

    def to_inner(l):
        return remote(part.at[l], r1.at[l], r1_send.at[l], r1_recv.at[l], {"mem": partner})

    def to_across(l):
        return remote(part.at[l], r2.at[l], r2_send.at[l], r2_recv.at[l], {"mem": across})

    def to_outer(l):
        return remote(tot.at[l], tot.at[l], t_send.at[l], t_recv.at[l], {"mem": partner})

    def out_grad(l):
        return pltpu.make_async_copy(av.at[:, l, 0:cols], grad.at[:, l], g_sem.at[l])

    def out_inc(l):
        return pltpu.make_async_copy(tot.at[l], inc.at[:, l], n_sem.at[l])

    innov_copy = pltpu.make_async_copy(innov, iv, i_sem)
    prec_copy = pltpu.make_async_copy(prec, pv, w_sem)

    barrier = pltpu.get_barrier_semaphore()
    for where in ({"tile": left}, {"tile": right}):
        pl.semaphore_signal(barrier, inc=1, device_id=where, device_id_type=MESH)
    for step in range(1, 4):
        pl.semaphore_signal(
            barrier, inc=1, device_id={"mem": lax.rem(z + step, 4)}, device_id_type=MESH
        )

    def load(l, carry):
        for copy in local(l):
            copy.start()
        return carry

    lax.fori_loop(0, levels, load, 0)
    innov_copy.start()
    prec_copy.start()
    pl.semaphore_wait(barrier, 5)

    def send_first(l, carry):
        for copy in diff_halo(l) + alpha_halo(l):
            copy.start()
        return carry

    lax.fori_loop(0, levels, send_first, 0)

    def coefficients(l):
        zonal, merid = dv[0, l], dv[1, l]
        lane = lax.broadcasted_iota(jnp.int32, merid.shape, 1)
        return zonal, jnp.where(lane < rows - 1, merid, 0.0)

    def forward(l):
        for copy in local(l):
            copy.wait()
        for copy in diff_halo(l) + alpha_halo(l):
            copy.wait_recv()
        zonal, merid = coefficients(l)
        part[l] = jnp.zeros(part.shape[1:], jnp.float32)

        def member(k, carry):
            localized = diffuse(av[k, l], zonal, merid)[0:cols]
            for slot in range(2):
                part[l, slot] += ev[slot, k, l].astype(jnp.float32) * localized
            return carry

        lax.fori_loop(0, members, member, 0)

        @pl.when(outer)
        def _():
            to_inner(l).start()

    def pair(l):
        @pl.when(inner)
        def _():
            to_inner(l).wait_recv()
            part[l] += r1[l]
            to_across(l).start()

    def total(l):
        @pl.when(inner)
        def _():
            to_across(l).wait_recv()
            tot[l] = part[l] + r2[l]
            to_outer(l).start()

    def project(l):
        @pl.when(outer)
        def _():
            to_outer(l).wait_recv()

        out_inc(l).start()
        weighted = [pv[slot, l] * (tot[l, slot] - iv[slot, l]) for slot in range(2)]

        def member(k, carry):
            pj[k, l, 0:cols] = (
                ev[0, k, l].astype(jnp.float32) * weighted[0]
                + ev[1, k, l].astype(jnp.float32) * weighted[1]
            )
            return carry

        lax.fori_loop(0, members, member, 0)
        for copy in proj_halo(l):
            copy.start()

    def adjoint(l):
        for copy in proj_halo(l):
            copy.wait_recv()
        zonal, merid = coefficients(l)

        def member(k, carry):
            av[k, l, 0:cols] += diffuse(pj[k, l], zonal, merid)[0:cols]
            return carry

        lax.fori_loop(0, members, member, 0)
        out_grad(l).start()

    def stage(work, step, lag):
        l = step - lag

        @pl.when((l >= 0) & (l < levels))
        def _():
            work(l)

    def step(s, carry):
        @pl.when(s == LAG_PROJECT)
        def _():
            innov_copy.wait()
            prec_copy.wait()

        stage(forward, s, 0)
        stage(pair, s, LAG_PAIR)
        stage(total, s, LAG_TOTAL)
        stage(project, s, LAG_PROJECT)
        stage(adjoint, s, LAG_ADJOINT)
        return carry

    lax.fori_loop(0, levels + LAG_ADJOINT, step, 0)

    def drain(l, carry):
        for copy in diff_halo(l) + alpha_halo(l) + proj_halo(l):
            copy.wait_send()

        @pl.when(outer)
        def _():
            to_inner(l).wait_send()

        @pl.when(inner)
        def _():
            to_across(l).wait_send()
            to_outer(l).wait_send()

        out_grad(l).wait()
        out_inc(l).wait()
        return carry

    lax.fori_loop(0, levels, drain, 0)


def per_device(tiles, alpha, ensemble, innovation, precision, diffusivity):
    members, levels, cols, rows = alpha.shape
    wide = cols + 2 * STEPS
    f32 = jnp.float32
    dma = pltpu.SemaphoreType.DMA
    slot = pltpu.VMEM((levels, 2, cols, rows), f32)
    return pl.pallas_call(
        functools.partial(kernel, tiles),
        out_shape=(
            jax.ShapeDtypeStruct(alpha.shape, f32),
            jax.ShapeDtypeStruct(innovation.shape, f32),
        ),
        in_specs=[pl.BlockSpec(memory_space=pl.ANY)] * 5,
        out_specs=(pl.BlockSpec(memory_space=pl.ANY), pl.BlockSpec(memory_space=pl.ANY)),
        scratch_shapes=[
            pltpu.VMEM((members, levels, wide, rows), f32),
            pltpu.VMEM(ensemble.shape, ensemble.dtype),
            pltpu.VMEM(innovation.shape, f32),
            pltpu.VMEM(precision.shape, f32),
            pltpu.VMEM((2, levels, wide, rows), f32),
            pltpu.VMEM((members, levels, wide, rows), f32),
            slot, slot, slot, slot,
            *[dma((2, levels))] * 6,
            *[dma((levels,))] * 6,
            *[dma((levels,))] * 3,
            dma, dma,
            dma((levels,)), dma((levels,)),
        ],
        compiler_params=pltpu.CompilerParams(collective_id=0, has_side_effects=True),
    )(alpha, ensemble, innovation, precision, diffusivity)


def solution(mesh):
    assert mesh.shape["mem"] == 4
    in_specs = (
        P("mem", None, "tile", None),
        P(None, "mem", None, "tile", None),
        P(None, None, "tile", None),
        P(None, None, "tile", None),
        P(None, None, "tile", None),
    )
    out_specs = (P("mem", None, "tile", None), P(None, None, "tile", None))
    return jax.shard_map(
        functools.partial(per_device, mesh.shape["tile"]),
        mesh=mesh, in_specs=in_specs, out_specs=out_specs, check_vma=False,
    )
```

```python
import functools

import jax
import jax.numpy as jnp
from jax import lax
from jax.experimental import pallas as pl
from jax.experimental.pallas import tpu as pltpu
from jax.sharding import PartitionSpec as P

STEPS = 4
UNROLL = 2
LAG_PAIR, LAG_TOTAL, LAG_PROJECT, LAG_ADJOINT = 1, 2, 4, 6
MESH = pl.DeviceIdType.MESH


def diffuse(field, center, east, west, north, south):
    columns, rows = field.shape[-2:]
    lead = field.ndim - 2
    for _ in range(STEPS):
        field = (
            center * field
            + (east * pltpu.roll(field, columns - 1, lead) + west * pltpu.roll(field, 1, lead))
            + (north * pltpu.roll(field, rows - 1, lead + 1) + south * pltpu.roll(field, 1, lead + 1))
        )
    return field


def kernel(
    tiles, alpha, ens, innov, prec, diff, grad, inc,
    av, ev, iv, pv, dv, pj, part, r1, r2, tot, cf,
    a_send, a_recv, d_send, d_recv, p_send, p_recv,
    r1_send, r1_recv, r2_send, r2_recv, t_send, t_recv,
    a_sem, e_sem, d_sem, i_sem, w_sem, g_sem, n_sem,
):
    members, levels, cols, rows = alpha.shape
    z = lax.axis_index("mem")
    t = lax.axis_index("tile")
    right, left = lax.rem(t + 1, tiles), lax.rem(t + tiles - 1, tiles)
    inner = (z == 1) | (z == 2)
    outer = (z == 0) | (z == 3)
    partner = z + 1 - 2 * lax.rem(z, 2)
    across = 3 - z

    def remote(src, dst, send, recv, where):
        return pltpu.make_async_remote_copy(
            src_ref=src, dst_ref=dst, send_sem=send, recv_sem=recv,
            device_id=where, device_id_type=MESH,
        )

    def halo(src, dst, send, recv, l):
        return (
            remote(src.at[:, l, 0:STEPS], dst.at[:, l, cols:cols + STEPS],
                   send.at[0, l], recv.at[0, l], {"tile": left}),
            remote(src.at[:, l, cols - STEPS:cols], dst.at[:, l, cols + STEPS:cols + 2 * STEPS],
                   send.at[1, l], recv.at[1, l], {"tile": right}),
        )

    def alpha_halo(l):
        return halo(alpha, av, a_send, a_recv, l)

    def diff_halo(l):
        return halo(diff, dv, d_send, d_recv, l)

    def proj_halo(l):
        return halo(pj, pj, p_send, p_recv, l)

    def local(l):
        return (
            pltpu.make_async_copy(diff.at[:, l], dv.at[:, l, 0:cols], d_sem.at[l]),
            pltpu.make_async_copy(alpha.at[:, l], av.at[:, l, 0:cols], a_sem.at[l]),
            pltpu.make_async_copy(ens.at[:, :, l], ev.at[:, :, l], e_sem.at[l]),
        )

    def to_inner(l):
        return remote(part.at[l], r1.at[l], r1_send.at[l], r1_recv.at[l], {"mem": partner})

    def to_across(l):
        return remote(part.at[l], r2.at[l], r2_send.at[l], r2_recv.at[l], {"mem": across})

    def to_outer(l):
        return remote(tot.at[l], tot.at[l], t_send.at[l], t_recv.at[l], {"mem": partner})

    def out_grad(l):
        return pltpu.make_async_copy(av.at[:, l, 0:cols], grad.at[:, l], g_sem.at[l])

    def out_inc(l):
        return pltpu.make_async_copy(tot.at[l], inc.at[:, l], n_sem.at[l])

    innov_copy = pltpu.make_async_copy(innov, iv, i_sem)
    prec_copy = pltpu.make_async_copy(prec, pv, w_sem)

    barrier = pltpu.get_barrier_semaphore()
    for where in ({"tile": left}, {"tile": right}):
        pl.semaphore_signal(barrier, inc=1, device_id=where, device_id_type=MESH)
    for step in range(1, 4):
        pl.semaphore_signal(
            barrier, inc=1, device_id={"mem": lax.rem(z + step, 4)}, device_id_type=MESH
        )

    def load(l, carry):
        for copy in local(l):
            copy.start()
        return carry

    lax.fori_loop(0, levels, load, 0)
    innov_copy.start()
    prec_copy.start()
    pl.semaphore_wait(barrier, 5)

    def send_first(l, carry):
        for copy in diff_halo(l) + alpha_halo(l):
            copy.start()
        return carry

    lax.fori_loop(0, levels, send_first, 0)

    def coefficients(l):
        east, merid = dv[0, l], dv[1, l]
        lane = lax.broadcasted_iota(jnp.int32, merid.shape, 1)
        north = jnp.where(lane < rows - 1, merid, 0.0)
        west, south = pltpu.roll(east, 1, 0), pltpu.roll(north, 1, 1)
        cf[0] = 1.0 - ((east + west) + (north + south))
        cf[1], cf[2], cf[3], cf[4] = east, west, north, south

    def spread(field):
        return diffuse(field, *[cf[i] for i in range(5)])

    def forward(l):
        for copy in local(l):
            copy.wait()
        for copy in diff_halo(l) + alpha_halo(l):
            copy.wait_recv()
        coefficients(l)
        part[l] = jnp.zeros(part.shape[1:], jnp.float32)

        def member(k, carry):
            localized = [spread(av[k * UNROLL + i, l])[0:cols] for i in range(UNROLL)]
            for slot in range(2):
                part[l, slot] += sum(
                    ev[slot, k * UNROLL + i, l].astype(jnp.float32) * localized[i]
                    for i in range(UNROLL)
                )
            return carry

        lax.fori_loop(0, members // UNROLL, member, 0)

        @pl.when(outer)
        def _():
            to_inner(l).start()

    def pair(l):
        @pl.when(inner)
        def _():
            to_inner(l).wait_recv()
            part[l] += r1[l]
            to_across(l).start()

    def total(l):
        @pl.when(inner)
        def _():
            to_across(l).wait_recv()
            tot[l] = part[l] + r2[l]
            to_outer(l).start()

    def project(l):
        @pl.when(outer)
        def _():
            to_outer(l).wait_recv()

        out_inc(l).start()
        weighted = [pv[slot, l] * (tot[l, slot] - iv[slot, l]) for slot in range(2)]

        def member(k, carry):
            pj[k, l, 0:cols] = (
                ev[0, k, l].astype(jnp.float32) * weighted[0]
                + ev[1, k, l].astype(jnp.float32) * weighted[1]
            )
            return carry

        lax.fori_loop(0, members, member, 0)
        for copy in proj_halo(l):
            copy.start()

    def adjoint(l):
        for copy in proj_halo(l):
            copy.wait_recv()
        coefficients(l)

        def member(k, carry):
            moved = [spread(pj[k * UNROLL + i, l])[0:cols] for i in range(UNROLL)]
            for i in range(UNROLL):
                av[k * UNROLL + i, l, 0:cols] += moved[i]
            return carry

        lax.fori_loop(0, members // UNROLL, member, 0)
        out_grad(l).start()

    def stage(work, step, lag):
        l = step - lag

        @pl.when((l >= 0) & (l < levels))
        def _():
            work(l)

    def step(s, carry):
        @pl.when(s == LAG_PROJECT)
        def _():
            innov_copy.wait()
            prec_copy.wait()

        stage(forward, s, 0)
        stage(pair, s, LAG_PAIR)
        stage(total, s, LAG_TOTAL)
        stage(project, s, LAG_PROJECT)
        stage(adjoint, s, LAG_ADJOINT)
        return carry

    lax.fori_loop(0, levels + LAG_ADJOINT, step, 0)

    def drain(l, carry):
        for copy in diff_halo(l) + alpha_halo(l) + proj_halo(l):
            copy.wait_send()

        @pl.when(outer)
        def _():
            to_inner(l).wait_send()

        @pl.when(inner)
        def _():
            to_across(l).wait_send()
            to_outer(l).wait_send()

        out_grad(l).wait()
        out_inc(l).wait()
        return carry

    lax.fori_loop(0, levels, drain, 0)


def per_device(tiles, alpha, ensemble, innovation, precision, diffusivity):
    members, levels, cols, rows = alpha.shape
    wide = cols + 2 * STEPS
    f32 = jnp.float32
    dma = pltpu.SemaphoreType.DMA
    slot = pltpu.VMEM((levels, 2, cols, rows), f32)
    return pl.pallas_call(
        functools.partial(kernel, tiles),
        out_shape=(
            jax.ShapeDtypeStruct(alpha.shape, f32),
            jax.ShapeDtypeStruct(innovation.shape, f32),
        ),
        in_specs=[pl.BlockSpec(memory_space=pl.ANY)] * 5,
        out_specs=(pl.BlockSpec(memory_space=pl.ANY), pl.BlockSpec(memory_space=pl.ANY)),
        scratch_shapes=[
            pltpu.VMEM((members, levels, wide, rows), f32),
            pltpu.VMEM(ensemble.shape, ensemble.dtype),
            pltpu.VMEM(innovation.shape, f32),
            pltpu.VMEM(precision.shape, f32),
            pltpu.VMEM((2, levels, wide, rows), f32),
            pltpu.VMEM((members, levels, wide, rows), f32),
            slot, slot, slot, slot,
            pltpu.VMEM((5, wide, rows), f32),
            *[dma((2, levels))] * 6,
            *[dma((levels,))] * 6,
            *[dma((levels,))] * 3,
            dma, dma,
            dma((levels,)), dma((levels,)),
        ],
        compiler_params=pltpu.CompilerParams(collective_id=0, has_side_effects=True),
    )(alpha, ensemble, innovation, precision, diffusivity)


def solution(mesh):
    assert mesh.shape["mem"] == 4
    in_specs = (
        P("mem", None, "tile", None),
        P(None, "mem", None, "tile", None),
        P(None, None, "tile", None),
        P(None, None, "tile", None),
        P(None, None, "tile", None),
    )
    out_specs = (P("mem", None, "tile", None), P(None, None, "tile", None))
    return jax.shard_map(
        functools.partial(per_device, mesh.shape["tile"]),
        mesh=mesh, in_specs=in_specs, out_specs=out_specs, check_vma=False,
    )
```

```python
import functools

import jax
import jax.numpy as jnp
from jax import lax
from jax.experimental import pallas as pl
from jax.experimental.pallas import tpu as pltpu
from jax.sharding import PartitionSpec as P

STEPS = 4
UNROLL = 4
LAG_PAIR, LAG_TOTAL, LAG_PROJECT, LAG_ADJOINT = 2, 4, 7, 9
MESH = pl.DeviceIdType.MESH


def diffuse(field, center, east, west, north, south):
    columns, rows = field.shape[-2:]
    lead = field.ndim - 2
    for _ in range(STEPS):
        field = (
            center * field
            + (east * pltpu.roll(field, columns - 1, lead) + west * pltpu.roll(field, 1, lead))
            + (north * pltpu.roll(field, rows - 1, lead + 1) + south * pltpu.roll(field, 1, lead + 1))
        )
    return field


def kernel(
    tiles, alpha, ens, innov, prec, diff, grad, inc,
    av, ev, iv, pv, dv, pj, part, r1, r2, tot, cf,
    a_send, a_recv, d_send, d_recv, p_send, p_recv,
    r1_send, r1_recv, r2_send, r2_recv, t_send, t_recv,
    a_sem, e_sem, d_sem, i_sem, w_sem,
):
    members, levels, cols, rows = alpha.shape
    z = lax.axis_index("mem")
    t = lax.axis_index("tile")
    right, left = lax.rem(t + 1, tiles), lax.rem(t + tiles - 1, tiles)
    inner = (z == 1) | (z == 2)
    outer = (z == 0) | (z == 3)
    partner = z + 1 - 2 * lax.rem(z, 2)
    across = 3 - z

    def remote(src, dst, send, recv, where):
        return pltpu.make_async_remote_copy(
            src_ref=src, dst_ref=dst, send_sem=send, recv_sem=recv,
            device_id=where, device_id_type=MESH,
        )

    def halo(src, dst, send, recv, l):
        return (
            remote(src.at[:, l, 0:STEPS], dst.at[:, l, cols:cols + STEPS],
                   send.at[0, l], recv.at[0, l], {"tile": left}),
            remote(src.at[:, l, cols - STEPS:cols], dst.at[:, l, cols + STEPS:cols + 2 * STEPS],
                   send.at[1, l], recv.at[1, l], {"tile": right}),
        )

    def alpha_halo(l):
        return halo(alpha, av, a_send, a_recv, l)

    def diff_halo(l):
        return halo(diff, dv, d_send, d_recv, l)

    def proj_halo(l):
        return halo(pj, pj, p_send, p_recv, l)

    def local(l):
        return (
            pltpu.make_async_copy(diff.at[:, l], dv.at[:, l, 0:cols], d_sem.at[l]),
            pltpu.make_async_copy(alpha.at[:, l], av.at[:, l, 0:cols], a_sem.at[l]),
            pltpu.make_async_copy(ens.at[:, :, l], ev.at[:, :, l], e_sem.at[l]),
        )

    def to_inner(l):
        return remote(part.at[l], r1.at[l], r1_send.at[l], r1_recv.at[l], {"mem": partner})

    def to_across(l):
        return remote(part.at[l], r2.at[l], r2_send.at[l], r2_recv.at[l], {"mem": across})

    def to_outer(l):
        return remote(tot.at[l], tot.at[l], t_send.at[l], t_recv.at[l], {"mem": partner})

    innov_copy = pltpu.make_async_copy(innov, iv, i_sem)
    prec_copy = pltpu.make_async_copy(prec, pv, w_sem)

    barrier = pltpu.get_barrier_semaphore()
    for where in ({"tile": left}, {"tile": right}):
        pl.semaphore_signal(barrier, inc=1, device_id=where, device_id_type=MESH)
    for step in range(1, 4):
        pl.semaphore_signal(
            barrier, inc=1, device_id={"mem": lax.rem(z + step, 4)}, device_id_type=MESH
        )

    def load(l, carry):
        for copy in local(l):
            copy.start()
        return carry

    lax.fori_loop(0, levels, load, 0)
    innov_copy.start()
    prec_copy.start()
    pl.semaphore_wait(barrier, 5)

    def send_first(l, carry):
        for copy in diff_halo(l) + alpha_halo(l):
            copy.start()
        return carry

    lax.fori_loop(0, levels, send_first, 0)

    def coefficients(l):
        east, merid = dv[0, l], dv[1, l]
        lane = lax.broadcasted_iota(jnp.int32, merid.shape, 1)
        north = jnp.where(lane < rows - 1, merid, 0.0)
        west, south = pltpu.roll(east, 1, 0), pltpu.roll(north, 1, 1)
        cf[l, 0] = 1.0 - ((east + west) + (north + south))
        cf[l, 1], cf[l, 2], cf[l, 3], cf[l, 4] = east, west, north, south

    def spread(field, l):
        return diffuse(field, *[cf[l, i] for i in range(5)])

    def forward(l):
        for copy in local(l):
            copy.wait()
        for copy in diff_halo(l) + alpha_halo(l):
            copy.wait_recv()
        coefficients(l)
        part[l] = jnp.zeros(part.shape[1:], jnp.float32)

        def member(k, carry):
            localized = [spread(av[k * UNROLL + i, l], l)[0:cols] for i in range(UNROLL)]
            for slot in range(2):
                part[l, slot] += sum(
                    ev[slot, k * UNROLL + i, l].astype(jnp.float32) * localized[i]
                    for i in range(UNROLL)
                )
            return carry

        lax.fori_loop(0, members // UNROLL, member, 0)

        @pl.when(outer)
        def _():
            to_inner(l).start()

    def pair(l):
        @pl.when(inner)
        def _():
            to_inner(l).wait_recv()
            part[l] += r1[l]
            to_across(l).start()

    def total(l):
        @pl.when(inner)
        def _():
            to_across(l).wait_recv()
            tot[l] = part[l] + r2[l]
            to_outer(l).start()

    def project(l):
        @pl.when(outer)
        def _():
            to_outer(l).wait_recv()

        inc[:, l] = tot[l]
        weighted = [pv[slot, l] * (tot[l, slot] - iv[slot, l]) for slot in range(2)]

        def member(k, carry):
            for i in range(4):
                pj[4 * k + i, l, 0:cols] = (
                    ev[0, 4 * k + i, l].astype(jnp.float32) * weighted[0]
                    + ev[1, 4 * k + i, l].astype(jnp.float32) * weighted[1]
                )
            return carry

        lax.fori_loop(0, members // 4, member, 0)
        for copy in proj_halo(l):
            copy.start()

    def adjoint(l):
        for copy in proj_halo(l):
            copy.wait_recv()

        def member(k, carry):
            moved = [spread(pj[k * UNROLL + i, l], l)[0:cols] for i in range(UNROLL)]
            for i in range(UNROLL):
                grad[k * UNROLL + i, l] = av[k * UNROLL + i, l, 0:cols] + moved[i]
            return carry

        lax.fori_loop(0, members // UNROLL, member, 0)

    def stage(work, step, lag):
        l = step - lag

        @pl.when((l >= 0) & (l < levels))
        def _():
            work(l)

    def step(s, carry):
        @pl.when(s == LAG_PROJECT)
        def _():
            innov_copy.wait()
            prec_copy.wait()

        stage(pair, s, LAG_PAIR)
        stage(total, s, LAG_TOTAL)
        stage(project, s, LAG_PROJECT)
        stage(forward, s, 0)
        stage(adjoint, s, LAG_ADJOINT)
        return carry

    lax.fori_loop(0, levels + LAG_ADJOINT, step, 0)

    def drain(l, carry):
        for copy in diff_halo(l) + alpha_halo(l) + proj_halo(l):
            copy.wait_send()

        @pl.when(outer)
        def _():
            to_inner(l).wait_send()

        @pl.when(inner)
        def _():
            to_across(l).wait_send()
            to_outer(l).wait_send()

        return carry

    lax.fori_loop(0, levels, drain, 0)


def per_device(tiles, alpha, ensemble, innovation, precision, diffusivity):
    members, levels, cols, rows = alpha.shape
    wide = cols + 2 * STEPS
    f32 = jnp.float32
    dma = pltpu.SemaphoreType.DMA
    slot = pltpu.VMEM((levels, 2, cols, rows), f32)
    return pl.pallas_call(
        functools.partial(kernel, tiles),
        out_shape=(pltpu.VMEM(alpha.shape, f32), pltpu.VMEM(innovation.shape, f32)),
        in_specs=[pl.BlockSpec(memory_space=pl.ANY)] * 5,
        out_specs=(pl.BlockSpec(memory_space=pltpu.VMEM), pl.BlockSpec(memory_space=pltpu.VMEM)),
        scratch_shapes=[
            pltpu.VMEM((members, levels, wide, rows), f32),
            pltpu.VMEM(ensemble.shape, ensemble.dtype),
            pltpu.VMEM(innovation.shape, f32),
            pltpu.VMEM(precision.shape, f32),
            pltpu.VMEM((2, levels, wide, rows), f32),
            pltpu.VMEM((members, levels, wide, rows), f32),
            slot, slot, slot, slot,
            pltpu.VMEM((levels, 5, wide, rows), f32),
            *[dma((2, levels))] * 6,
            *[dma((levels,))] * 6,
            *[dma((levels,))] * 3,
            dma, dma,
        ],
        compiler_params=pltpu.CompilerParams(collective_id=0, has_side_effects=True),
    )(alpha, ensemble, innovation, precision, diffusivity)


def solution(mesh):
    assert mesh.shape["mem"] == 4
    in_specs = (
        P("mem", None, "tile", None),
        P(None, "mem", None, "tile", None),
        P(None, None, "tile", None),
        P(None, None, "tile", None),
        P(None, None, "tile", None),
    )
    out_specs = (P("mem", None, "tile", None), P(None, None, "tile", None))
    return jax.shard_map(
        functools.partial(per_device, mesh.shape["tile"]),
        mesh=mesh, in_specs=in_specs, out_specs=out_specs, check_vma=False,
    )
```

```python
import functools

import jax
import jax.numpy as jnp
from jax import lax
from jax.experimental import pallas as pl
from jax.experimental.pallas import tpu as pltpu
from jax.sharding import PartitionSpec as P

STEPS = 4
UNROLL = 4
LAG_PAIR, LAG_TOTAL, LAG_PROJECT, LAG_ADJOINT = 2, 4, 7, 9
MESH = pl.DeviceIdType.MESH


def diffuse(field, center, east, west, north, south):
    columns, rows = field.shape[-2:]
    lead = field.ndim - 2
    for _ in range(STEPS):
        field = (
            center * field
            + (east * pltpu.roll(field, columns - 1, lead) + west * pltpu.roll(field, 1, lead))
            + (north * pltpu.roll(field, rows - 1, lead + 1) + south * pltpu.roll(field, 1, lead + 1))
        )
    return field


def kernel(
    tiles, alpha, ens, innov, prec, diff, grad, inc,
    av, ev, iv, pv, dv, pj, part, r1, r2, tot, cf,
    a_send, a_recv, d_send, d_recv, p_send, p_recv,
    r1_send, r1_recv, r2_send, r2_recv, t_send, t_recv,
    a_sem, e_sem, d_sem, i_sem, w_sem,
):
    members, levels, cols, rows = alpha.shape
    z = lax.axis_index("mem")
    t = lax.axis_index("tile")
    right, left = lax.rem(t + 1, tiles), lax.rem(t + tiles - 1, tiles)
    inner = (z == 1) | (z == 2)
    outer = (z == 0) | (z == 3)
    partner = z + 1 - 2 * lax.rem(z, 2)
    across = 3 - z

    def remote(src, dst, send, recv, where):
        return pltpu.make_async_remote_copy(
            src_ref=src, dst_ref=dst, send_sem=send, recv_sem=recv,
            device_id=where, device_id_type=MESH,
        )

    def halo(src, dst, send, recv, l):
        return (
            remote(src.at[:, l, 0:STEPS], dst.at[:, l, cols:cols + STEPS],
                   send.at[0, l], recv.at[0, l], {"tile": left}),
            remote(src.at[:, l, cols - STEPS:cols], dst.at[:, l, cols + STEPS:cols + 2 * STEPS],
                   send.at[1, l], recv.at[1, l], {"tile": right}),
        )

    def alpha_halo(l):
        return halo(alpha, av, a_send, a_recv, l)

    def diff_halo(l):
        return halo(diff, dv, d_send, d_recv, l)

    def proj_halo(l):
        return halo(pj, pj, p_send, p_recv, l)

    def local(l):
        return (
            pltpu.make_async_copy(diff.at[:, l], dv.at[:, l, 0:cols], d_sem.at[l]),
            pltpu.make_async_copy(alpha.at[:, l], av.at[:, l, 0:cols], a_sem.at[l]),
            pltpu.make_async_copy(ens.at[:, :, l], ev.at[:, :, l], e_sem.at[l]),
        )

    def to_inner(l):
        return remote(part.at[l], r1.at[l], r1_send.at[l], r1_recv.at[l], {"mem": partner})

    def to_across(l):
        return remote(part.at[l], r2.at[l], r2_send.at[l], r2_recv.at[l], {"mem": across})

    def to_outer(l):
        return remote(tot.at[l], tot.at[l], t_send.at[l], t_recv.at[l], {"mem": partner})

    innov_copy = pltpu.make_async_copy(innov, iv, i_sem)
    prec_copy = pltpu.make_async_copy(prec, pv, w_sem)

    barrier = pltpu.get_barrier_semaphore()
    for where in ({"tile": left}, {"tile": right}):
        pl.semaphore_signal(barrier, inc=1, device_id=where, device_id_type=MESH)
    pl.semaphore_signal(barrier, inc=1, device_id={"mem": partner}, device_id_type=MESH)

    @pl.when(inner)
    def _():
        pl.semaphore_signal(barrier, inc=1, device_id={"mem": across}, device_id_type=MESH)

    def load(l, carry):
        for copy in local(l):
            copy.start()
        return carry

    lax.fori_loop(0, levels, load, 0)
    innov_copy.start()
    prec_copy.start()

    @pl.when(inner)
    def _():
        pl.semaphore_wait(barrier, 4)

    @pl.when(outer)
    def _():
        pl.semaphore_wait(barrier, 3)

    def send_first(l, carry):
        for copy in diff_halo(l) + alpha_halo(l):
            copy.start()
        return carry

    lax.fori_loop(0, levels, send_first, 0)

    def coefficients(l):
        east, merid = dv[0, l], dv[1, l]
        lane = lax.broadcasted_iota(jnp.int32, merid.shape, 1)
        north = jnp.where(lane < rows - 1, merid, 0.0)
        west, south = pltpu.roll(east, 1, 0), pltpu.roll(north, 1, 1)
        cf[l, 0] = 1.0 - ((east + west) + (north + south))
        cf[l, 1], cf[l, 2], cf[l, 3], cf[l, 4] = east, west, north, south

    def spread(field, l):
        return diffuse(field, *[cf[l, i] for i in range(5)])

    def forward(l):
        for copy in local(l):
            copy.wait()
        for copy in diff_halo(l) + alpha_halo(l):
            copy.wait_recv()
        coefficients(l)
        part[l] = jnp.zeros(part.shape[1:], jnp.float32)

        def member(k, carry):
            localized = [spread(av[k * UNROLL + i, l], l)[0:cols] for i in range(UNROLL)]
            for slot in range(2):
                part[l, slot] += sum(
                    ev[slot, k * UNROLL + i, l].astype(jnp.float32) * localized[i]
                    for i in range(UNROLL)
                )
            return carry

        lax.fori_loop(0, members // UNROLL, member, 0)

        @pl.when(outer)
        def _():
            to_inner(l).start()

    def pair(l):
        @pl.when(inner)
        def _():
            to_inner(l).wait_recv()
            part[l] += r1[l]
            to_across(l).start()

    def total(l):
        @pl.when(inner)
        def _():
            to_across(l).wait_recv()
            tot[l] = part[l] + r2[l]
            to_outer(l).start()

    def project(l):
        @pl.when(outer)
        def _():
            to_outer(l).wait_recv()

        inc[:, l] = tot[l]
        weighted = [pv[slot, l] * (tot[l, slot] - iv[slot, l]) for slot in range(2)]

        def member(k, carry):
            for i in range(8):
                pj[8 * k + i, l, 0:cols] = (
                    ev[0, 8 * k + i, l].astype(jnp.float32) * weighted[0]
                    + ev[1, 8 * k + i, l].astype(jnp.float32) * weighted[1]
                )
            return carry

        lax.fori_loop(0, members // 8, member, 0)
        for copy in proj_halo(l):
            copy.start()

    def adjoint(l):
        for copy in proj_halo(l):
            copy.wait_recv()

        def member(k, carry):
            moved = [spread(pj[k * UNROLL + i, l], l)[0:cols] for i in range(UNROLL)]
            for i in range(UNROLL):
                grad[k * UNROLL + i, l] = av[k * UNROLL + i, l, 0:cols] + moved[i]
            return carry

        lax.fori_loop(0, members // UNROLL, member, 0)

    def stage(work, step, lag):
        l = step - lag

        @pl.when((l >= 0) & (l < levels))
        def _():
            work(l)

    def step(s, carry):
        @pl.when(s == LAG_PROJECT)
        def _():
            innov_copy.wait()
            prec_copy.wait()

        stage(total, s, LAG_TOTAL)
        stage(pair, s, LAG_PAIR)
        stage(project, s, LAG_PROJECT)
        stage(forward, s, 0)
        stage(adjoint, s, LAG_ADJOINT)
        return carry

    lax.fori_loop(0, levels + LAG_ADJOINT, step, 0)

    def drain(l, carry):
        for copy in diff_halo(l) + alpha_halo(l) + proj_halo(l):
            copy.wait_send()

        @pl.when(outer)
        def _():
            to_inner(l).wait_send()

        @pl.when(inner)
        def _():
            to_across(l).wait_send()
            to_outer(l).wait_send()

        return carry

    lax.fori_loop(0, levels, drain, 0)


def per_device(tiles, alpha, ensemble, innovation, precision, diffusivity):
    members, levels, cols, rows = alpha.shape
    wide = cols + 2 * STEPS
    f32 = jnp.float32
    dma = pltpu.SemaphoreType.DMA
    slot = pltpu.VMEM((levels, 2, cols, rows), f32)
    return pl.pallas_call(
        functools.partial(kernel, tiles),
        out_shape=(pltpu.VMEM(alpha.shape, f32), pltpu.VMEM(innovation.shape, f32)),
        in_specs=[pl.BlockSpec(memory_space=pl.ANY)] * 5,
        out_specs=(pl.BlockSpec(memory_space=pltpu.VMEM), pl.BlockSpec(memory_space=pltpu.VMEM)),
        scratch_shapes=[
            pltpu.VMEM((members, levels, wide, rows), f32),
            pltpu.VMEM(ensemble.shape, ensemble.dtype),
            pltpu.VMEM(innovation.shape, f32),
            pltpu.VMEM(precision.shape, f32),
            pltpu.VMEM((2, levels, wide, rows), f32),
            pltpu.VMEM((members, levels, wide, rows), f32),
            slot, slot, slot, slot,
            pltpu.VMEM((levels, 5, wide, rows), f32),
            *[dma((2, levels))] * 6,
            *[dma((levels,))] * 6,
            *[dma((levels,))] * 3,
            dma, dma,
        ],
        compiler_params=pltpu.CompilerParams(collective_id=0, has_side_effects=True),
    )(alpha, ensemble, innovation, precision, diffusivity)


def solution(mesh):
    assert mesh.shape["mem"] == 4
    in_specs = (
        P("mem", None, "tile", None),
        P(None, "mem", None, "tile", None),
        P(None, None, "tile", None),
        P(None, None, "tile", None),
        P(None, None, "tile", None),
    )
    out_specs = (P("mem", None, "tile", None), P(None, None, "tile", None))
    return jax.shard_map(
        functools.partial(per_device, mesh.shape["tile"]),
        mesh=mesh, in_specs=in_specs, out_specs=out_specs, check_vma=False,
    )
```
